256 devices in a mesh: blk: 64 (over y_hi, x, z), freq: 4 (over y_lo, core).
Axes of the slice: x: 4, y: 4 (y_hi: 2, y_lo: 2; y = y_hi * 2 + y_lo), z: 8, core: 2. Of those that a mesh axis runs over, the one named last changes fastest.
Arguments:
- spectra: bfloat16 [2, 128, 8192, 512], P(None, 'freq', 'blk'), may hold values from -6 to 6
- halfwidth: int32 [8192], P('blk'), may hold values from 1 to 3
Outputs:
- cross: bfloat16 [2, 2, 128, 8192, 128], P(None, None, 'freq', 'blk')
The draws below stay inside these ranges and needn't reach their ends.
All inputs are finite; a program needn't handle non-finite values.
Results may differ from the reference program's by a relative error of at most 0.0064.
Values may be sent and summed in bfloat16 or wider, within the bound.
No kernel may reach another device: no remote copies, remote signals or barrier semaphores. Data moves between devices by JAX's collectives and lax.ppermute only.
A program may use at most 128 MiB of HBM per device.

```python
import jax
import jax.numpy as jnp
from jax import lax

CB = 128
W = 512
F = 128
HMAX = 3
ROUNDS = 2
C = 8192
N_BLK = 64


def set_ends(array, rng, smallest, top_value):
    extent = array.shape
    index_at = [jax.random.randint(jax.random.fold_in(rng, axis), (), 0, extent[axis]) for axis in range(len(extent))]
    array = array.at[tuple(index_at)].set(smallest)
    longest = extent.index(max(extent))
    index_at[longest] = (index_at[longest] + 1) % extent[longest]
    return array.at[tuple(index_at)].set(top_value)


def shard_levels(key, dims, cuts, smallest, top_value):
    def one(axis_at, shards_of):
        heights = jax.random.uniform(jax.random.fold_in(jax.random.fold_in(key, 6), axis_at), (shards_of,), jnp.float32, smallest / len(cuts), top_value / len(cuts))
        return jnp.repeat(jnp.exp(heights), dims[axis_at] // shards_of).reshape((-1,) + (1,) * (len(dims) - axis_at - 1))

    loudness = one(*cuts[0])
    for cut in cuts[1:]:
        loudness = loudness * one(*cut)
    return loudness


def bell_draw(rng, extent, deviation, reach, pieces=(), kind=jnp.bfloat16):
    entries = deviation * jax.random.normal(rng, extent, jnp.float32)
    if pieces:
        entries = entries * shard_levels(rng, extent, pieces, -0.22, 0.18)
    return jnp.clip(entries, -reach, reach).astype(kind)


def setup_inputs(seed: int = 0) -> dict:
    splits = jax.random.split(jax.random.key(seed), 3)
    spectra = bell_draw(splits[0], (2, F, C, W), 1.0, 6.0, ((1, 4), (2, 64)))
    halfwidth = set_ends(jax.random.randint(splits[1], (C,), 1, HMAX + 1), jax.random.fold_in(splits[1], 1), 1, HMAX).astype(jnp.int32)
    return {"spectra": spectra, "halfwidth": halfwidth}


def whiten_all(block, widths):
    real_part = block[0].astype(jnp.float32)
    imag_part = block[1].astype(jnp.float32)
    energy = real_part * real_part + imag_part * imag_part
    padded = jnp.pad(energy, ((HMAX, HMAX), (0, 0), (0, 0)))
    bin_index = jnp.arange(F, dtype=jnp.int32)
    smooth = jnp.zeros_like(energy)
    counts = jnp.zeros((F, CB), jnp.float32)
    for offset in range(-HMAX, HMAX + 1):
        inside = abs(offset) <= widths
        in_grid = (bin_index + offset >= 0) & (bin_index + offset < F)
        weight = (inside[None, :] & in_grid[:, None]).astype(jnp.float32)
        smooth = smooth + weight[:, :, None] * padded[offset + HMAX:offset + HMAX + F]
        counts = counts + weight
    root_mean = jnp.sqrt(smooth / counts[:, :, None])
    factor = 1.0 / jnp.maximum(root_mean, 0.5)
    return jnp.stack((real_part * factor, imag_part * factor)).astype(jnp.bfloat16)

def cross_sums(own_block, partner):
    own_real = own_block[0].astype(jnp.float32)
    own_imag = own_block[1].astype(jnp.float32)
    par_real = partner[0].astype(jnp.float32)
    par_imag = partner[1].astype(jnp.float32)
    real_sum = jnp.einsum('fcw,fdw->fcd', own_real, par_real) + jnp.einsum('fcw,fdw->fcd', own_imag, par_imag)
    imag_sum = jnp.einsum('fcw,fdw->fcd', own_imag, par_real) - jnp.einsum('fcw,fdw->fcd', own_real, par_imag)
    return jnp.stack((real_sum, imag_sum)).astype(jnp.bfloat16)

def reference(spectra, halfwidth):
    blocks = jnp.moveaxis(spectra.reshape(2, F, N_BLK, CB, W), 2, 0)
    widths = halfwidth.reshape(N_BLK, CB)
    whitened = lax.map(lambda pair: whiten_all(pair[0], pair[1]), (blocks, widths))
    half_len = W // 2
    tile_list = []
    for round_index in range(ROUNDS):
        flip = N_BLK >> round_index + 1

        def single(index):
            own_block = whitened[index]
            partner = whitened[index ^ flip]
            first = cross_sums(own_block[..., :half_len], partner[..., :half_len])
            second = cross_sums(own_block[..., half_len:], partner[..., half_len:])
            summed = first.astype(jnp.float32) + second.astype(jnp.float32)
            return (summed * W ** (-0.5)).astype(jnp.bfloat16)
        tiles = lax.map(single, jnp.arange(N_BLK, dtype=jnp.int32))
        tile_list.append(jnp.moveaxis(tiles, 0, 2).reshape(2, F, N_BLK * CB, CB))
    return jnp.stack(tile_list)
```

```python
import functools

import jax
import jax.numpy as jnp
from jax import lax
from jax.experimental import pallas as pl
from jax.experimental.pallas import tpu as pltpu
from jax.sharding import PartitionSpec as P

CB = 128
W = 512
F = 128
HMAX = 3
SPLITS = (2, 4, 5, 5)
ROWS = 16
GROUPS = 4


def bin_of(q, k, half):
    return jnp.where(q == 0, half + k, half - 1 - k)


def edge_kernel(info, keep_in, send_in, keep_out, send_out):
    for src, dst in ((keep_in, keep_out), (send_in, send_out)):
        re = src[0, 0].astype(jnp.float32)
        im = src[1, 0].astype(jnp.float32)
        dst[0] = (re * re + im * im).astype(jnp.bfloat16)


def edge_energies(info, spectra):
    bins = spectra.shape[1]
    half = bins // 2
    block = (2, 1, CB, W)
    out = jax.ShapeDtypeStruct((HMAX, CB, W), jnp.bfloat16)
    return pl.pallas_call(
        edge_kernel,
        out_shape=(out, out),
        grid_spec=pltpu.PrefetchScalarGridSpec(
            num_scalar_prefetch=1,
            grid=(HMAX,),
            in_specs=[
                pl.BlockSpec(block, lambda i, info: (0, bin_of(1 - info[0], half - 1 - i, half), 0, 0)),
                pl.BlockSpec(block, lambda i, info: (0, bin_of(info[0], half - 1 - i, half), 0, 0)),
            ],
            out_specs=[
                pl.BlockSpec((1, CB, W), lambda i, info: (i, 0, 0)),
                pl.BlockSpec((1, CB, W), lambda i, info: (i, 0, 0)),
            ],
        ),
        name="edge",
    )(info, spectra, spectra)


def whiten_kernel(info, spectra, widths, *rest, k0, n, half, keep, with_halo):
    if with_halo:
        halo, out, raw, sems = rest
    else:
        out, raw, sems = rest
    q = 1 - info[0] if keep else info[0]
    base = info[1] * (2 * half)
    low = k0 - HMAX
    high = min(k0 + n + HMAX, half)
    held = high - low
    start = jnp.where(q == 0, half + low, half - high)
    rows = CB // GROUPS

    def copy(group):
        part = pl.ds(group * rows, rows)
        return pltpu.make_async_copy(
            spectra.at[:, pl.ds(start, held), part, :], raw.at[:, :, part, :], sems.at[group]
        )

    for group in range(GROUPS):
        copy(group).start()
    for group in range(GROUPS):
        copy(group).wait()

        def unit(step, _, group=group):
            row = pl.multiple_of(group * rows + step * ROWS, ROWS)
            part = pl.ds(row, ROWS)
            width = widths[part, :]
            two = width >= 2.0
            three = width >= 3.0
            inverse = []
            for k in range(k0, k0 + n):
                g = (base + bin_of(q, k, half)).astype(jnp.float32)
                count = jnp.minimum(width, g) + jnp.minimum(width, F - 1.0 - g) + 1.0
                inverse.append(1.0 / count)
            for lane in range(0, W, 128):
                cols = slice(lane, lane + 128)
                res, ims, energy = [], [], []
                for k in range(low, k0 + n + HMAX):
                    if k < half:
                        at = jnp.where(q == 0, k - low, high - 1 - k)
                        re = raw[0, at, part, cols].astype(jnp.float32)
                        im = raw[1, at, part, cols].astype(jnp.float32)
                        res.append(re)
                        ims.append(im)
                        energy.append(re * re + im * im)
                    else:
                        energy.append(halo[k - half, part, cols].astype(jnp.float32))
                for i in range(n):
                    c = i + HMAX
                    near = energy[c] + (energy[c - 1] + energy[c + 1])
                    mid = energy[c - 2] + energy[c + 2]
                    far = energy[c - 3] + energy[c + 3]
                    smooth = near + jnp.where(two, mid, 0.0) + jnp.where(three, far, 0.0)
                    factor = lax.rsqrt(jnp.maximum(smooth * inverse[i], 0.25))
                    re = (res[c] * factor).astype(jnp.bfloat16)
                    im = (ims[c] * factor).astype(jnp.bfloat16)
                    right = slice(W + lane, W + lane + 128)
                    out[i, part, cols] = re
                    out[i, part, right] = im
                    if keep:
                        lower = pl.ds(row + CB, ROWS)
                        out[i, lower, cols] = im
                        out[i, lower, right] = -re
            return 0

        lax.fori_loop(0, rows // ROWS, unit, 0)


def whiten(info, spectra, widths, halo, k0, n, keep):
    half = spectra.shape[1] // 2
    with_halo = k0 + n + HMAX > half
    held = min(k0 + n + HMAX, half) - k0 + HMAX
    operands = [info, spectra, widths] + ([halo] if with_halo else [])
    vmem = pl.BlockSpec(memory_space=pltpu.VMEM)
    return pl.pallas_call(
        functools.partial(whiten_kernel, k0=k0, n=n, half=half, keep=keep, with_halo=with_halo),
        out_shape=jax.ShapeDtypeStruct((n, 2 * CB if keep else CB, 2 * W), jnp.bfloat16),
        in_specs=[pl.BlockSpec(memory_space=pltpu.SMEM), pl.BlockSpec(memory_space=pl.ANY), vmem]
        + ([vmem] if with_halo else []),
        out_specs=vmem,
        scratch_shapes=[
            pltpu.VMEM((2, held, CB, W), jnp.bfloat16),
            pltpu.SemaphoreType.DMA((GROUPS,)),
        ],
        name=("keep" if keep else "send") + str(k0),
    )(*operands)


def tile_kernel(info, own, first, second, *rest):
    out, back_first, back_second = rest[-3:]
    contract = (((1,), (1,)), ((), ()))
    a = own[0]
    b = jnp.concatenate([first[0], second[0]], axis=0)
    scale = W ** (-0.5)
    ahead = lax.dot_general(a, b, contract, preferred_element_type=jnp.float32) * scale
    for r in range(2):
        for part in range(2):
            tile = ahead[part * CB:(part + 1) * CB, r * CB:(r + 1) * CB]
            out[r, part, 0] = tile.astype(jnp.bfloat16)
    turned = lax.dot_general(b, a, contract, preferred_element_type=jnp.float32) * scale
    for r, back in enumerate((back_first, back_second)):
        back[0, 0] = turned[r * CB:(r + 1) * CB, :CB].astype(jnp.bfloat16)
        back[1, 0] = (-turned[r * CB:(r + 1) * CB, CB:]).astype(jnp.bfloat16)


def tiles(info, own, first, second, out, k0, n, bins):
    half = bins // 2
    back = jax.ShapeDtypeStruct((2, n, CB, CB), jnp.bfloat16)
    back_spec = pl.BlockSpec((2, 1, CB, CB), lambda i, info: (0, jnp.where(info[0] == 1, i, n - 1 - i), 0, 0))
    got_spec = pl.BlockSpec((1, CB, 2 * W), lambda i, info: (i, 0, 0))
    operands = [info, own, first, second] + ([] if out is None else [out])
    return pl.pallas_call(
        tile_kernel,
        out_shape=(jax.ShapeDtypeStruct((2, 2, bins, CB, CB), jnp.bfloat16), back, back),
        grid_spec=pltpu.PrefetchScalarGridSpec(
            num_scalar_prefetch=1,
            grid=(n,),
            in_specs=[
                pl.BlockSpec((1, 2 * CB, 2 * W), lambda i, info: (i, 0, 0)),
                got_spec,
                got_spec,
            ]
            + ([] if out is None else [pl.BlockSpec(memory_space=pl.ANY)]),
            out_specs=[
                pl.BlockSpec((2, 2, 1, CB, CB), lambda i, info: (0, 0, bin_of(1 - info[0], k0 + i, half), 0, 0)),
                back_spec,
                back_spec,
            ],
        ),
        input_output_aliases={} if out is None else {4: 0},
        name="tiles" + str(k0),
    )(*operands)


def place_kernel(info, first, second, _, out, sems, *, k0, n, half):
    start = jnp.where(info[0] == 0, half + k0, half - k0 - n)
    copies = [
        pltpu.make_async_copy(got, out.at[r, :, pl.ds(start, n)], sems.at[r])
        for r, got in enumerate((first, second))
    ]
    for copy in copies:
        copy.start()
    for copy in copies:
        copy.wait()


def place(info, first, second, out, k0, n):
    any_spec = pl.BlockSpec(memory_space=pl.ANY)
    return pl.pallas_call(
        functools.partial(place_kernel, k0=k0, n=n, half=out.shape[2] // 2),
        out_shape=jax.ShapeDtypeStruct(out.shape, out.dtype),
        in_specs=[pl.BlockSpec(memory_space=pltpu.SMEM), any_spec, any_spec, any_spec],
        out_specs=any_spec,
        scratch_shapes=[pltpu.SemaphoreType.DMA((2,))],
        input_output_aliases={3: 0},
        name="place" + str(k0),
    )(info, first, second, out)


def per_device(spectra, halfwidth):
    bins = spectra.shape[1]
    blocks = lax.axis_size("blk")
    shards = lax.axis_size("freq")
    flips = (blocks >> 1, blocks >> 2)

    def parity(b):
        return (b // flips[0] + b // flips[1]) % 2

    block = lax.axis_index("blk")
    info = jnp.stack([parity(block), lax.axis_index("freq")]).astype(jnp.int32)
    widths = jnp.broadcast_to(halfwidth.astype(jnp.float32)[:, None], (CB, 128))

    def swap(value, r):
        return lax.ppermute(value, "blk", [(i, i ^ flips[r]) for i in range(blocks)])

    def shift(value, steps):
        pairs = []
        for b in range(blocks):
            step = steps[parity(b)]
            for f in range(shards):
                if 0 <= f + step < shards:
                    pairs.append((b * shards + f, b * shards + f + step))
        return lax.ppermute(value, ("blk", "freq"), pairs)

    spans = []
    at = 0
    for n in SPLITS:
        spans.append((at, n))
        at += n

    k0, n = spans[0]
    sent = whiten(info, spectra, widths, None, k0, n, False)
    got = [(swap(sent, 0), swap(sent, 1))]
    keep_edge, send_edge = edge_energies(info, spectra)
    send_halo = shift(keep_edge, (-1, 1))
    keep_halo = shift(send_edge, (1, -1))
    for k0, n in spans[1:]:
        sent = whiten(info, spectra, widths, send_halo, k0, n, False)
        got.append((swap(sent, 0), swap(sent, 1)))
    kept = [whiten(info, spectra, widths, keep_halo, k0, n, True) for k0, n in spans]

    out = None
    returned = []
    for (k0, n), own, (first, second) in zip(spans, kept, got):
        out, back_first, back_second = tiles(info, own, first, second, out, k0, n, bins)
        returned.append((swap(back_first, 0), swap(back_second, 1)))
    for (k0, n), (first, second) in zip(spans, returned):
        out = place(info, first, second, out, k0, n)
    return out


def solution(mesh):
    return jax.shard_map(
        per_device,
        mesh=mesh,
        in_specs=(P(None, "freq", "blk", None), P("blk")),
        out_specs=P(None, None, "freq", "blk", None),
        check_vma=False,
    )
```
